32 devices in a mesh: dp: 8 (over y, x, core), mp: 4 (over z).
Axes of the slice: x: 2, y: 2, z: 4, core: 2. Of those that a mesh axis runs over, the one named last changes fastest.
Arguments:
- tokens: bfloat16 [2048, 1024], P('dp'), may hold values from -6 to 6
- norm_gain1: float32 [1024], replicated, may hold values from 0.25 to 1.75
- in_weight: bfloat16 [1024, 3, 1024], P(None, None, 'mp'), may hold values from -0.1875 to 0.1875
- conv_taps: float32 [3, 1024], P(None, 'mp'), may hold values from -3 to 3
- out_weight: bfloat16 [1024, 1024], P('mp'), may hold values from -0.1875 to 0.1875
- norm_gain2: float32 [1024], replicated, may hold values from 0.25 to 1.75
- gate_weight: bfloat16 [1024, 4608], P(None, 'mp'), may hold values from -0.1875 to 0.1875
- up_weight: bfloat16 [1024, 4608], P(None, 'mp'), may hold values from -0.1875 to 0.1875
- down_weight: bfloat16 [4608, 1024], P('mp'), may hold values from -0.09375 to 0.09375
- cotangent: bfloat16 [2048, 1024], P('dp'), may hold values from -6 to 6
Outputs:
- block_out: bfloat16 [2048, 1024], P('dp')
- input_grad: bfloat16 [2048, 1024], P('dp')
- grad_gain1: float32 [1024], replicated
- grad_in: float32 [1024, 3, 1024], P('dp', None, 'mp')
- grad_taps: float32 [3, 1024], P(None, 'mp')
- grad_out: float32 [1024, 1024], P('mp', 'dp')
- grad_gain2: float32 [1024], replicated
- grad_gate: float32 [1024, 4608], P('dp', 'mp')
- grad_up: float32 [1024, 4608], P('dp', 'mp')
- grad_down: float32 [4608, 1024], P('mp', 'dp')
The draws below stay inside these ranges and needn't reach their ends.
All inputs are finite; a program needn't handle non-finite values.
Results may differ from the reference program's by a relative error of at most 0.0098.
Values sent between devices are 32-bit elements; how exact they have to be, the bound alone decides.
A program may use at most 128 MiB of HBM per device.

```python
import jax
import jax.numpy as jnp
from jax import lax

D = 1024
FF = 4608
KERNEL = 3
SEQ = 256
TOKENS = 2048


def raised(entries, own_key, source, target, parts, factor):
    owner, partner = [(jnp.arange(entries.shape[position]) // (entries.shape[position] // parts)).reshape([-1 if axis == position else 1 for axis in range(entries.ndim)]) for position in (source, target)]
    chosen = jax.random.permutation(own_key, parts)[partner]
    strong = (owner == chosen) | (owner == (partner + parts // 2) % parts)
    return jnp.where(strong, factor * entries, entries)


def block_levels(key, dims, shards, least, high):
    level, own = 1.0, jax.random.fold_in(key, 6)
    for axis_at, blocks in shards:
        draws = jnp.exp(jax.random.uniform(jax.random.fold_in(own, axis_at), (blocks,), jnp.float32, least / len(shards), high / len(shards)))
        level = level * jnp.repeat(draws, dims[axis_at] // blocks).reshape([-1 if axis == axis_at else 1 for axis in range(len(dims))])
    return level


def normal_values(own_key, shape, deviation, limit, cuts=(), dtype=jnp.bfloat16):
    array = jax.random.normal(own_key, shape, jnp.float32) * deviation
    if len(cuts) > 0:
        array = block_levels(own_key, shape, cuts, -0.22, 0.18) * array
    return jnp.clip(array, min=-limit, max=limit).astype(dtype)


def gaussian_with(key, dims, deviation, limit, split, heavy, dtype=jnp.bfloat16):
    values = deviation * jax.random.normal(key, dims, jnp.float32)
    if split:
        values = values * block_levels(key, dims, split, -0.22, 0.18)
    return jnp.clip(raised(values, jax.random.fold_in(key, 3), *heavy), -limit, limit).astype(dtype)


def setup_inputs(seed: int = 0) -> dict:
    arg_keys = jax.random.split(jax.random.key(seed), 11)
    return {
        "tokens": normal_values(arg_keys[0], (TOKENS, D), 1.0, 6.0, ((0, 8),)),
        "norm_gain1": jnp.clip(1.0 + 0.15 * jax.random.normal(arg_keys[1], (D,), jnp.float32), 0.25, 1.75),
        "in_weight": normal_values(arg_keys[2], (D, 3, D), D ** -0.5, 0.1875, ((2, 4),)),
        "conv_taps": normal_values(arg_keys[3], (KERNEL, D), 0.6, 3.0, ((1, 4),), jnp.float32),
        "out_weight": normal_values(arg_keys[4], (D, D), D ** -0.5, 0.1875, ((0, 4),)),
        "norm_gain2": jnp.clip(1.0 + 0.15 * jax.random.normal(arg_keys[5], (D,), jnp.float32), 0.25, 1.75),
        "gate_weight": normal_values(arg_keys[6], (D, FF), D ** -0.5, 0.1875, ((1, 4),)),
        "up_weight": normal_values(arg_keys[7], (D, FF), D ** -0.5, 0.1875, ((1, 4),)),
        "down_weight": normal_values(arg_keys[8], (FF, D), FF ** -0.5, 0.09375, ((0, 4),)),
        "cotangent": gaussian_with(arg_keys[9], (TOKENS, D), 1.0, 6.0, ((0, 8),), (0, 1, 8, 2.0)),
    }


epsilon = 1e-05

def rms_forward(values, norm_gain):
    inverse = lax.rsqrt(lax.optimization_barrier(jnp.mean(values * values, axis=-1, keepdims=True)) + epsilon)
    unit = values * inverse
    return (unit, inverse, (unit * norm_gain).astype(jnp.bfloat16))

def rms_backward(grad_normed, unit, inverse, norm_gain):
    grad_gain = lax.optimization_barrier(jnp.sum(grad_normed * unit, axis=0))
    scaled = grad_normed * norm_gain
    grad_values = inverse * (scaled - unit * lax.optimization_barrier(jnp.mean(scaled * unit, axis=-1, keepdims=True)))
    return (grad_values, grad_gain)

def lagged(values, offset):
    return jnp.pad(values, ((offset, 0), (0, 0)))[:values.shape[0]]

def leading(values, offset):
    return jnp.pad(values, ((0, offset), (0, 0)))[offset:]

def conv_forward(mixed, conv_taps):
    total = jnp.zeros(mixed.shape, jnp.float32)
    for offset in range(conv_taps.shape[0]):
        total = total + conv_taps[offset] * lagged(mixed, offset)
    return total

def conv_backward(grad_conv, mixed, conv_taps):
    grad_mixed = jnp.zeros(mixed.shape, jnp.float32)
    rows_list = []
    for offset in range(conv_taps.shape[0]):
        grad_mixed = grad_mixed + conv_taps[offset] * leading(grad_conv, offset)
        rows_list.append(lax.optimization_barrier(jnp.sum(grad_conv * lagged(mixed, offset), axis=0)))
    return (grad_mixed, jnp.stack(rows_list))

def reference(tokens, norm_gain1, in_weight, conv_taps, out_weight, norm_gain2, gate_weight, up_weight, down_weight, cotangent):
    width = tokens.shape[1]
    in_flat = in_weight.reshape(width, -1)
    streams = in_weight.shape[1] * in_weight.shape[2]

    def per_sequence(totals, pieces):
        inputs_bf, upstream = pieces
        inputs = inputs_bf.astype(jnp.float32)
        length = inputs.shape[0]
        unit1, inverse1, normed1 = rms_forward(inputs, norm_gain1)
        proj = jnp.dot(normed1, in_flat, preferred_element_type=jnp.float32).reshape(length, 3, -1)
        gate_b = proj[:, 0]
        gate_c = proj[:, 1]
        stream_x = proj[:, 2]
        mixed = gate_b * stream_x
        conved = conv_forward(mixed, conv_taps)
        gated = (gate_c * conved).astype(jnp.bfloat16)
        resid = inputs + jnp.dot(gated, out_weight, preferred_element_type=jnp.float32)
        unit2, inverse2, normed2 = rms_forward(resid, norm_gain2)
        gate_pre = jnp.dot(normed2, gate_weight, preferred_element_type=jnp.float32)
        up_pre = jnp.dot(normed2, up_weight, preferred_element_type=jnp.float32)
        sigmoid_gate = jax.nn.sigmoid(gate_pre)
        silu_gate = gate_pre * sigmoid_gate
        hidden = (silu_gate * up_pre).astype(jnp.bfloat16)
        block_out = (resid + jnp.dot(hidden, down_weight, preferred_element_type=jnp.float32)).astype(jnp.bfloat16)
        grad_down = jnp.dot(hidden.T, upstream, preferred_element_type=jnp.float32)
        grad_hidden = jnp.dot(upstream, down_weight.T, preferred_element_type=jnp.float32)
        grad_gpre = (grad_hidden * up_pre * sigmoid_gate * (1.0 + gate_pre * (1.0 - sigmoid_gate))).astype(jnp.bfloat16)
        grad_upre = (grad_hidden * silu_gate).astype(jnp.bfloat16)
        grad_gate = jnp.dot(normed2.T, grad_gpre, preferred_element_type=jnp.float32)
        grad_up = jnp.dot(normed2.T, grad_upre, preferred_element_type=jnp.float32)
        grad_norm2 = jnp.dot(grad_gpre, gate_weight.T, preferred_element_type=jnp.float32) + jnp.dot(grad_upre, up_weight.T, preferred_element_type=jnp.float32)
        grad_from2, grad_gain2 = rms_backward(grad_norm2, unit2, inverse2, norm_gain2)
        grad_resid = upstream.astype(jnp.float32) + grad_from2
        resid_bf = grad_resid.astype(jnp.bfloat16)
        grad_out = jnp.dot(gated.T, resid_bf, preferred_element_type=jnp.float32)
        grad_gated = jnp.dot(resid_bf, out_weight.T, preferred_element_type=jnp.float32)
        grad_c = grad_gated * conved
        grad_conv = grad_gated * gate_c
        grad_mixed, grad_taps = conv_backward(grad_conv, mixed, conv_taps)
        grad_proj = jnp.stack([grad_mixed * stream_x, grad_c, grad_mixed * gate_b], axis=1).astype(jnp.bfloat16).reshape(length, streams)
        grad_in = jnp.dot(normed1.T, grad_proj, preferred_element_type=jnp.float32)
        grad_norm1 = jnp.dot(grad_proj, in_flat.T, preferred_element_type=jnp.float32)
        grad_from1, grad_gain1 = rms_backward(grad_norm1, unit1, inverse1, norm_gain1)
        input_grad = (grad_resid + grad_from1).astype(jnp.bfloat16)
        terms = (grad_gain1, grad_in, grad_taps, grad_out, grad_gain2, grad_gate, grad_up, grad_down)
        updated = tuple((old + new for old, new in zip(totals, terms)))
        return (updated, (block_out, input_grad))
    initial = (jnp.zeros((width,), jnp.float32), jnp.zeros((width, streams), jnp.float32), jnp.zeros(conv_taps.shape, jnp.float32), jnp.zeros(out_weight.shape, jnp.float32), jnp.zeros((width,), jnp.float32), jnp.zeros(gate_weight.shape, jnp.float32), jnp.zeros(up_weight.shape, jnp.float32), jnp.zeros(down_weight.shape, jnp.float32))
    sequences = tokens.reshape(-1, SEQ, width)
    upstreams = cotangent.reshape(-1, SEQ, width)
    totals, (outputs, gradients) = lax.scan(per_sequence, initial, (sequences, upstreams))
    return (outputs.reshape(-1, width), gradients.reshape(-1, width), totals[0], totals[1].reshape(in_weight.shape), totals[2], totals[3], totals[4], totals[5], totals[6], totals[7])
```

```python
import functools

import jax
import jax.numpy as jnp
from jax import lax
from jax.experimental import pallas as pl
from jax.experimental.pallas import tpu as pltpu
from jax.sharding import PartitionSpec as P

epsilon = 1e-05
MESH = pl.DeviceIdType.MESH
CHUNKS = 16


def remote(src, dst, send, recv, axis, index):
    return pltpu.make_async_remote_copy(
        src_ref=src,
        dst_ref=dst,
        send_sem=send,
        recv_sem=recv,
        device_id={axis: index},
        device_id_type=MESH,
    )


class LineSum:
    def __init__(self, part, out, near, across, total, sems):
        self.part, self.out = part, out
        self.near, self.across, self.total = near, across, total
        self.sems = sems
        self.me = lax.axis_index("mp")
        self.rows = part.shape[0] // CHUNKS

    def at(self, ref, k):
        return ref.at[pl.ds(k * self.rows, self.rows), :]

    def inward(self, k):
        return remote(
            self.at(self.part, k), self.at(self.near, k),
            self.sems.at[0, k], self.sems.at[1, k], "mp", 1 + self.me // 3,
        )

    def swap(self, k):
        return remote(
            self.at(self.near, k), self.at(self.across, k),
            self.sems.at[2, k], self.sems.at[3, k], "mp", 3 - self.me,
        )

    def outward(self, k):
        return remote(
            self.at(self.total, k), self.at(self.total, k),
            self.sems.at[4, k], self.sems.at[5, k], "mp", (3 * self.me + 1) % 4,
        )

    def end_start(self):
        for k in range(CHUNKS):
            self.inward(k).start()

    def middle_step(self, k):
        self.inward(k).wait_recv()
        rows = pl.ds(k * self.rows, self.rows)
        self.near[rows, :] = self.near[rows, :] + self.part[rows, :]
        self.swap(k).start()

    def middle_close(self, k):
        self.swap(k).wait_recv()
        rows = pl.ds(k * self.rows, self.rows)
        self.total[rows, :] = self.near[rows, :] + self.across[rows, :]
        self.outward(k).start()
        self.out[rows, :] = self.total[rows, :]

    def end_finish(self):
        for k in range(CHUNKS):
            self.outward(k).wait_recv()
            rows = pl.ds(k * self.rows, self.rows)
            self.out[rows, :] = self.total[rows, :]
        for k in range(CHUNKS):
            self.inward(k).wait_send()

    def middle_finish(self):
        for k in range(CHUNKS):
            self.swap(k).wait_send()
            self.outward(k).wait_send()


class BlockSum:
    def __init__(self, full, out, first, second, third, sends, recvs, by_rows, start, size):
        self.full, self.out = full, out
        self.first, self.second, self.third = first, second, third
        self.sends, self.recvs = sends, recvs
        self.by_rows, self.start, self.size = by_rows, start, size
        me = lax.axis_index("dp")
        self.y, self.x, self.c = me // 4, (me // 2) % 2, me % 2
        self.to_core = me + 1 - 2 * self.c
        self.to_x = me + 2 - 4 * self.x
        self.to_y = me + 4 - 8 * self.y
        self.block = first.shape[1]
        self.half = self.block // 2

    def source(self, j):
        if self.by_rows:
            return (pl.ds(pl.multiple_of(j * self.block, self.block), self.block), pl.ds(self.start, self.size))
        width = self.first.shape[2]
        return (pl.ds(self.start, self.size), pl.ds(pl.multiple_of(j * width, width), width))

    def target(self, h):
        if self.by_rows:
            return (pl.ds(h * self.half, self.half), pl.ds(self.start, self.size))
        return (pl.ds(self.start + h * self.half, self.half), slice(None))

    def part(self, h):
        return pl.ds(h * self.half, self.half)

    def copy0(self, q):
        return remote(
            self.full.at[self.source(2 * q + 1 - self.c)], self.first.at[q],
            self.sends.at[q], self.recvs.at[q], "dp", self.to_core,
        )

    def copy1(self, n):
        if n < 2:
            src, dst = self.first.at[2 * n + 1 - self.x, self.part(0)], self.to_x
        else:
            src, dst = self.first.at[2 * (1 - self.y) + n - 2, self.part(1)], self.to_y
        return remote(src, self.second.at[n], self.sends.at[4 + n], self.recvs.at[4 + n], "dp", dst)

    def copy2(self, h):
        if h == 0:
            src, dst = self.second.at[1 - self.y], self.to_y
        else:
            src, dst = self.second.at[3 - self.x], self.to_x
        return remote(src, self.third.at[h], self.sends.at[8 + h], self.recvs.at[8 + h], "dp", dst)

    def stage0(self):
        for q in range(4):
            self.copy0(q).start()

    def stage1(self):
        for q in range(4):
            self.copy0(q).wait_recv()
            self.first[q] = self.first[q] + self.full[self.source(2 * q + self.c)]
        for n in (0, 2, 1, 3):
            self.copy1(n).start()

    def stage2(self):
        for n in range(4):
            self.copy1(n).wait_recv()
            if n < 2:
                mine = self.first[2 * n + self.x, self.part(0)]
            else:
                mine = self.first[2 * self.y + n - 2, self.part(1)]
            self.second[n] = self.second[n] + mine
        for h in range(2):
            self.copy2(h).start()

    def finish(self):
        for h in range(2):
            self.copy2(h).wait_recv()
            mine = self.second[self.y] if h == 0 else self.second[2 + self.x]
            self.out[self.target(h)] = mine + self.third[h]

    def drain(self):
        for q in range(4):
            self.copy0(q).wait_send()
            self.copy1(q).wait_send()
        for h in range(2):
            self.copy2(h).wait_send()


def greet(with_blocks):
    barrier = pltpu.get_barrier_semaphore()
    mp, dp = lax.axis_index("mp"), lax.axis_index("dp")
    middle = (mp == 1) | (mp == 2)

    def hello(axis, index):
        pl.semaphore_signal(barrier, inc=1, device_id={axis: index}, device_id_type=MESH)

    if with_blocks:
        y, x, c = dp // 4, (dp // 2) % 2, dp % 2
        hello("dp", dp + 1 - 2 * c)
        hello("dp", dp + 2 - 4 * x)
        hello("dp", dp + 4 - 8 * y)

    @pl.when(middle)
    def _():
        hello("mp", 3 - mp)
        hello("mp", 3 * (mp - 1))
        pl.semaphore_wait(barrier, 5 if with_blocks else 2)

    @pl.when(jnp.logical_not(middle))
    def _():
        hello("mp", 1 + mp // 3)
        pl.semaphore_wait(barrier, 4 if with_blocks else 1)

    return middle


def traffic_kernel(n_sums, n_blocks, items, *refs):
    refs = list(refs)
    take = lambda n: [refs.pop(0) for _ in range(n)]
    parts, fulls = take(n_sums), take(n_blocks)
    outs, shards = take(n_sums), take(n_blocks)
    line_scratch = [take(4) for _ in range(n_sums)]
    item_scratch = [take(5) for _ in items]
    middle = greet(n_blocks > 0)
    sums = [LineSum(p, o, *s) for p, o, s in zip(parts, outs, line_scratch)]
    blocks = [
        BlockSum(fulls[which], shards[which], *scratch, by_rows, start, size)
        for (which, by_rows, start, size), scratch in zip(items, item_scratch)
    ]

    @pl.when(jnp.logical_not(middle))
    def _():
        for one in sums:
            one.end_start()

    for block in blocks[:2]:
        block.stage0()
    for block in blocks[2:]:
        block.stage0()

    steps = [(one, k) for one in sums for k in range(CHUNKS)]
    actions = []
    for t in range(len(steps) + 2):
        actions.append((steps[t] if t < len(steps) else None, steps[t - 2] if t >= 2 else None))

    def run(batch):
        @pl.when(middle)
        def _():
            for opening, closing in batch:
                if opening is not None:
                    opening[0].middle_step(opening[1])
                if closing is not None:
                    closing[0].middle_close(closing[1])

    slots = []
    count = len(blocks)
    for t in range(count + 2):
        if t < count:
            slots.append(blocks[t].stage1)
        if 1 <= t and t - 1 < count:
            slots.append(blocks[t - 1].stage2)
        if 2 <= t:
            slots.append(blocks[t - 2].finish)
    if not slots:
        run(actions)
    else:
        done = 0
        for position, slot in enumerate(slots):
            slot()
            upto = -(-len(actions) * (position + 1) // len(slots))
            if upto > done:
                run(actions[done:upto])
                done = upto

    @pl.when(middle)
    def _():
        for one in sums:
            one.middle_finish()

    @pl.when(jnp.logical_not(middle))
    def _():
        for one in sums:
            one.end_finish()

    for block in blocks:
        block.drain()


def traffic(partials, fulls, items, collective_id):
    f32 = jnp.float32
    scratch = []
    for p in partials:
        scratch += [pltpu.VMEM(p.shape, f32)] * 3 + [pltpu.SemaphoreType.DMA((6, CHUNKS))]
    sent = sum(p.size for p in partials) * 4
    for which, by_rows, _, size in items:
        full = fulls[which]
        r, c = (full.shape[0] // 8, size) if by_rows else (size, full.shape[1] // 8)
        scratch += [
            pltpu.VMEM((4, r, c), f32),
            pltpu.VMEM((4, r // 2, c), f32),
            pltpu.VMEM((2, r // 2, c), f32),
            pltpu.SemaphoreType.DMA((10,)),
            pltpu.SemaphoreType.DMA((10,)),
        ]
        sent += 7 * r * c * 4
    kinds = {which: by_rows for which, by_rows, _, _ in items}
    shards = [
        jax.ShapeDtypeStruct(
            (f.shape[0] // 8, f.shape[1]) if kinds[i] else (f.shape[0], f.shape[1] // 8), f32
        )
        for i, f in enumerate(fulls)
    ]
    vmem = pl.BlockSpec(memory_space=pltpu.VMEM)
    n_in = len(partials) + len(fulls)
    return pl.pallas_call(
        functools.partial(traffic_kernel, len(partials), len(fulls), items),
        out_shape=[jax.ShapeDtypeStruct(p.shape, f32) for p in partials] + shards,
        in_specs=[vmem] * n_in,
        out_specs=[vmem] * n_in,
        scratch_shapes=scratch,
        compiler_params=pltpu.CompilerParams(
            collective_id=collective_id, has_side_effects=True, vmem_limit_bytes=60 * 1024 * 1024
        ),
        name=f"traffic_{collective_id}",
    )(*partials, *fulls)


def small_kernel(n, x_ref, o_ref, held, sends, recvs):
    me = lax.axis_index("dp")
    barrier = pltpu.get_barrier_semaphore()
    for s in range(1, n):
        pl.semaphore_signal(barrier, inc=1, device_id={"dp": lax.rem(me + s, n)}, device_id_type=MESH)
    pl.semaphore_wait(barrier, n - 1)

    def copy(s):
        return remote(x_ref, held.at[me], sends.at[s], recvs.at[s], "dp", lax.rem(me + s, n))

    for s in range(1, n):
        copy(s).start()
    held[me] = x_ref[...]
    for s in range(1, n):
        copy(s).wait_recv()
    total = held[0]
    for i in range(1, n):
        total = total + held[i]
    o_ref[...] = total
    for s in range(1, n):
        copy(s).wait_send()


def small_sum(n, x, collective_id):
    vmem = pl.BlockSpec(memory_space=pltpu.VMEM)
    return pl.pallas_call(
        functools.partial(small_kernel, n),
        out_shape=jax.ShapeDtypeStruct(x.shape, x.dtype),
        in_specs=[vmem],
        out_specs=vmem,
        scratch_shapes=[
            pltpu.VMEM((n, *x.shape), x.dtype),
            pltpu.SemaphoreType.DMA((n,)),
            pltpu.SemaphoreType.DMA((n,)),
        ],
        compiler_params=pltpu.CompilerParams(collective_id=collective_id, has_side_effects=True),
        name="small_sum",
    )(x)


def split_rows(which, size, pieces):
    return [(which, False, i * (size // pieces), size // pieces) for i in range(pieces)]


def split_columns(which, size, pieces):
    lanes = size // 128
    edges = [i * lanes // pieces * 128 for i in range(pieces)] + [size]
    return [(which, True, a, b - a) for a, b in zip(edges, edges[1:])]


def rms_forward(values, norm_gain):
    inverse = lax.rsqrt(jnp.mean(values * values, axis=-1, keepdims=True) + epsilon)
    unit = values * inverse
    return (unit, inverse, (unit * norm_gain).astype(jnp.bfloat16))


def rms_backward(grad_normed, unit, inverse, norm_gain):
    grad_gain = jnp.sum(grad_normed * unit, axis=0)
    scaled = grad_normed * norm_gain
    grad_values = inverse * (scaled - unit * jnp.mean(scaled * unit, axis=-1, keepdims=True))
    return (grad_values, grad_gain)


def lagged(values, offset):
    return jnp.pad(values, ((offset, 0), (0, 0)))[: values.shape[0]]


def leading(values, offset):
    return jnp.pad(values, ((0, offset), (0, 0)))[offset:]


def conv_forward(mixed, conv_taps):
    total = jnp.zeros(mixed.shape, jnp.float32)
    for offset in range(conv_taps.shape[0]):
        total = total + conv_taps[offset] * lagged(mixed, offset)
    return total


def conv_backward(grad_conv, mixed, conv_taps):
    grad_mixed = jnp.zeros(mixed.shape, jnp.float32)
    rows_list = []
    for offset in range(conv_taps.shape[0]):
        grad_mixed = grad_mixed + conv_taps[offset] * leading(grad_conv, offset)
        rows_list.append(jnp.sum(grad_conv * lagged(mixed, offset), axis=0))
    return (grad_mixed, jnp.stack(rows_list))


def sums_over_mp(fast, partials, collective_id):
    if fast:
        return traffic(partials, [], [], collective_id)
    return [lax.psum(p, "mp") for p in partials]


def body(
    parts,
    groups,
    tokens,
    norm_gain1,
    in_weight,
    conv_taps,
    out_weight,
    norm_gain2,
    gate_weight,
    up_weight,
    down_weight,
    cotangent,
):
    length = tokens.shape[0]
    width = tokens.shape[1]
    in_flat = in_weight.reshape(width, -1)
    streams = in_flat.shape[1]
    inputs = tokens.astype(jnp.float32)
    unit1, inverse1, normed1 = rms_forward(inputs, norm_gain1)
    proj = jnp.dot(normed1, in_flat, preferred_element_type=jnp.float32).reshape(length, 3, -1)
    gate_b = proj[:, 0]
    gate_c = proj[:, 1]
    stream_x = proj[:, 2]
    mixed = gate_b * stream_x
    conved = conv_forward(mixed, conv_taps)
    gated = (gate_c * conved).astype(jnp.bfloat16)
    fast = parts == 8 and groups == 4
    (branch,) = sums_over_mp(
        fast, [jnp.dot(gated, out_weight, preferred_element_type=jnp.float32)], 0
    )
    resid = inputs + branch
    unit2, inverse2, normed2 = rms_forward(resid, norm_gain2)
    gate_pre = jnp.dot(normed2, gate_weight, preferred_element_type=jnp.float32)
    up_pre = jnp.dot(normed2, up_weight, preferred_element_type=jnp.float32)
    sigmoid_gate = jax.nn.sigmoid(gate_pre)
    silu_gate = gate_pre * sigmoid_gate
    hidden = (silu_gate * up_pre).astype(jnp.bfloat16)
    partial_ffn = jnp.dot(hidden, down_weight, preferred_element_type=jnp.float32)
    grad_down = jnp.dot(hidden.T, cotangent, preferred_element_type=jnp.float32)
    grad_hidden = jnp.dot(cotangent, down_weight.T, preferred_element_type=jnp.float32)
    grad_gpre = (
        grad_hidden * up_pre * sigmoid_gate * (1.0 + gate_pre * (1.0 - sigmoid_gate))
    ).astype(jnp.bfloat16)
    grad_upre = (grad_hidden * silu_gate).astype(jnp.bfloat16)
    grad_gate = jnp.dot(normed2.T, grad_gpre, preferred_element_type=jnp.float32)
    grad_up = jnp.dot(normed2.T, grad_upre, preferred_element_type=jnp.float32)
    partial_norm2 = jnp.dot(grad_gpre, gate_weight.T, preferred_element_type=jnp.float32) + jnp.dot(
        grad_upre, up_weight.T, preferred_element_type=jnp.float32
    )
    if fast:
        grad_norm2, ffn_out, summed_down, summed_gate, summed_up = traffic(
            [partial_norm2, partial_ffn],
            [grad_down, grad_gate, grad_up],
            split_rows(0, grad_down.shape[0], 2)
            + split_columns(1, grad_gate.shape[1], 2)
            + split_columns(2, grad_up.shape[1], 2),
            1,
        )
    else:
        grad_norm2, ffn_out = lax.psum((partial_norm2, partial_ffn), "mp")
        summed_down = lax.psum_scatter(grad_down, "dp", scatter_dimension=1, tiled=True)
        summed_gate = lax.psum_scatter(grad_gate, "dp", scatter_dimension=0, tiled=True)
        summed_up = lax.psum_scatter(grad_up, "dp", scatter_dimension=0, tiled=True)
    block_out = (resid + ffn_out).astype(jnp.bfloat16)
    grad_from2, grad_gain2 = rms_backward(grad_norm2, unit2, inverse2, norm_gain2)
    grad_resid = cotangent.astype(jnp.float32) + grad_from2
    resid_bf = grad_resid.astype(jnp.bfloat16)
    grad_out = jnp.dot(gated.T, resid_bf, preferred_element_type=jnp.float32)
    grad_gated = jnp.dot(resid_bf, out_weight.T, preferred_element_type=jnp.float32)
    grad_c = grad_gated * conved
    grad_conv = grad_gated * gate_c
    grad_mixed, grad_taps = conv_backward(grad_conv, mixed, conv_taps)
    grad_proj = (
        jnp.stack([grad_mixed * stream_x, grad_c, grad_mixed * gate_b], axis=1)
        .astype(jnp.bfloat16)
        .reshape(length, streams)
    )
    grad_in = jnp.dot(normed1.T, grad_proj, preferred_element_type=jnp.float32)
    partial_norm1 = jnp.dot(grad_proj, in_flat.T, preferred_element_type=jnp.float32)
    if fast:
        grad_norm1, summed_in, summed_out = traffic(
            [partial_norm1],
            [grad_in, grad_out],
            split_columns(0, grad_in.shape[1], 2) + split_rows(1, grad_out.shape[0], 1),
            2,
        )
    else:
        grad_norm1 = lax.psum(partial_norm1, "mp")
        summed_in = lax.psum_scatter(grad_in, "dp", scatter_dimension=0, tiled=True)
        summed_out = lax.psum_scatter(grad_out, "dp", scatter_dimension=1, tiled=True)
    grad_from1, grad_gain1 = rms_backward(grad_norm1, unit1, inverse1, norm_gain1)
    input_grad = (grad_resid + grad_from1).astype(jnp.bfloat16)
    if fast:
        small = jnp.concatenate(
            [grad_gain1.reshape(-1, 128), grad_gain2.reshape(-1, 128), grad_taps.reshape(-1, 128)]
        )
        count = small.shape[0]
        small = small_sum(parts, jnp.pad(small, ((0, -count % 8), (0, 0))), 3)
        rows = width // 128
        total_gain1 = small[:rows].reshape(-1)
        total_gain2 = small[rows : 2 * rows].reshape(-1)
        total_taps = small[2 * rows : count].reshape(grad_taps.shape)
    else:
        total_gain1, total_taps, total_gain2 = lax.psum((grad_gain1, grad_taps, grad_gain2), "dp")
    return (
        block_out,
        input_grad,
        total_gain1,
        summed_in.reshape(summed_in.shape[0], 3, -1),
        total_taps,
        summed_out,
        total_gain2,
        summed_gate,
        summed_up,
        summed_down,
    )


def solution(mesh):
    in_specs = (
        P("dp", None),
        P(),
        P(None, None, "mp"),
        P(None, "mp"),
        P("mp", None),
        P(),
        P(None, "mp"),
        P(None, "mp"),
        P("mp", None),
        P("dp", None),
    )
    out_specs = (
        P("dp", None),
        P("dp", None),
        P(),
        P("dp", None, "mp"),
        P(None, "mp"),
        P("mp", "dp"),
        P(),
        P("dp", "mp"),
        P("dp", "mp"),
        P("mp", "dp"),
    )
    local = functools.partial(body, mesh.shape["dp"], mesh.shape["mp"])
    return jax.shard_map(local, mesh=mesh, in_specs=in_specs, out_specs=out_specs, check_vma=False)
```

```python
import functools

import jax
import jax.numpy as jnp
from jax import lax
from jax.experimental import pallas as pl
from jax.experimental.pallas import tpu as pltpu
from jax.sharding import PartitionSpec as P

epsilon = 1e-05
MESH = pl.DeviceIdType.MESH
CHUNK_ROWS = 16


def remote(src, dst, send, recv, axis, index):
    return pltpu.make_async_remote_copy(
        src_ref=src,
        dst_ref=dst,
        send_sem=send,
        recv_sem=recv,
        device_id={axis: index},
        device_id_type=MESH,
    )


class LineSum:
    def __init__(self, part, out, near, across, total, sems):
        self.part, self.out = part, out
        self.near, self.across, self.total = near, across, total
        self.sems = sems
        self.me = lax.axis_index("mp")
        self.rows = CHUNK_ROWS
        self.chunks = part.shape[0] // CHUNK_ROWS

    def at(self, ref, k):
        return ref.at[pl.ds(k * self.rows, self.rows), :]

    def inward(self, k):
        return remote(
            self.at(self.part, k), self.at(self.near, k),
            self.sems.at[0, k], self.sems.at[1, k], "mp", 1 + self.me // 3,
        )

    def swap(self, k):
        return remote(
            self.at(self.near, k), self.at(self.across, k),
            self.sems.at[2, k], self.sems.at[3, k], "mp", 3 - self.me,
        )

    def outward(self, k):
        return remote(
            self.at(self.total, k), self.at(self.total, k),
            self.sems.at[4, k], self.sems.at[5, k], "mp", (3 * self.me + 1) % 4,
        )

    def end_start(self):
        for k in range(self.chunks):
            self.inward(k).start()

    def middle_step(self, k):
        self.inward(k).wait_recv()
        rows = pl.ds(k * self.rows, self.rows)
        self.near[rows, :] = self.near[rows, :] + self.part[rows, :]
        self.swap(k).start()

    def middle_close(self, k):
        self.swap(k).wait_recv()
        rows = pl.ds(k * self.rows, self.rows)
        self.total[rows, :] = self.near[rows, :] + self.across[rows, :]
        self.outward(k).start()
        self.out[rows, :] = self.total[rows, :]

    def end_finish(self):
        for k in range(self.chunks):
            self.outward(k).wait_recv()
            rows = pl.ds(k * self.rows, self.rows)
            self.out[rows, :] = self.total[rows, :]
        for k in range(self.chunks):
            self.inward(k).wait_send()

    def middle_finish(self):
        for k in range(self.chunks):
            self.swap(k).wait_send()
            self.outward(k).wait_send()


class BlockSum:
    def __init__(self, left, right, out, mine, first, second, third, sends, recvs, by_rows, start, size):
        self.left, self.right, self.out, self.mine = left, right, out, mine
        self.first, self.second, self.third = first, second, third
        self.sends, self.recvs = sends, recvs
        self.by_rows, self.start, self.size = by_rows, start, size
        me = lax.axis_index("dp")
        self.y, self.x, self.c = me // 4, (me // 2) % 2, me % 2
        self.to_core = me + 1 - 2 * self.c
        self.to_x = me + 2 - 4 * self.x
        self.to_y = me + 4 - 8 * self.y
        self.block = first.shape[1]
        self.half = self.block // 2

    def produce(self, j):
        if self.by_rows:
            rows = pl.ds(pl.multiple_of(j * self.block, self.block), self.block)
            columns = pl.ds(self.start, self.size)
        else:
            width = self.first.shape[2]
            rows = pl.ds(self.start, self.size)
            columns = pl.ds(pl.multiple_of(j * width, width), width)
        return jnp.dot(self.left[rows, :], self.right[:, columns], preferred_element_type=jnp.float32)

    def target(self, h):
        if self.by_rows:
            return (pl.ds(h * self.half, self.half), pl.ds(self.start, self.size))
        return (pl.ds(self.start + h * self.half, self.half), slice(None))

    def part(self, h):
        return pl.ds(h * self.half, self.half)

    def copy0(self, q):
        return remote(
            self.mine.at[q], self.first.at[q],
            self.sends.at[q], self.recvs.at[q], "dp", self.to_core,
        )

    def copy1(self, n):
        if n < 2:
            src, dst = self.first.at[2 * n + 1 - self.x, self.part(0)], self.to_x
        else:
            src, dst = self.first.at[2 * (1 - self.y) + n - 2, self.part(1)], self.to_y
        return remote(src, self.second.at[n], self.sends.at[4 + n], self.recvs.at[4 + n], "dp", dst)

    def copy2(self, h):
        if h == 0:
            src, dst = self.second.at[1 - self.y], self.to_y
        else:
            src, dst = self.second.at[3 - self.x], self.to_x
        return remote(src, self.third.at[h], self.sends.at[8 + h], self.recvs.at[8 + h], "dp", dst)

    def stage0(self):
        for q in range(4):
            self.mine[q] = self.produce(2 * q + 1 - self.c)
            self.copy0(q).start()

    def stage1(self):
        for q in range(4):
            self.copy0(q).wait_recv()
            self.first[q] = self.first[q] + self.produce(2 * q + self.c)
        for n in (0, 2, 1, 3):
            self.copy1(n).start()

    def stage2(self):
        for n in range(4):
            self.copy1(n).wait_recv()
            if n < 2:
                mine = self.first[2 * n + self.x, self.part(0)]
            else:
                mine = self.first[2 * self.y + n - 2, self.part(1)]
            self.second[n] = self.second[n] + mine
        for h in range(2):
            self.copy2(h).start()

    def finish(self):
        for h in range(2):
            self.copy2(h).wait_recv()
            mine = self.second[self.y] if h == 0 else self.second[2 + self.x]
            self.out[self.target(h)] = mine + self.third[h]

    def drain(self):
        for q in range(4):
            self.copy0(q).wait_send()
            self.copy1(q).wait_send()
        for h in range(2):
            self.copy2(h).wait_send()


def greet(with_blocks):
    barrier = pltpu.get_barrier_semaphore()
    mp, dp = lax.axis_index("mp"), lax.axis_index("dp")
    middle = (mp == 1) | (mp == 2)

    def hello(axis, index):
        pl.semaphore_signal(barrier, inc=1, device_id={axis: index}, device_id_type=MESH)

    if with_blocks:
        y, x, c = dp // 4, (dp // 2) % 2, dp % 2
        hello("dp", dp + 1 - 2 * c)
        hello("dp", dp + 2 - 4 * x)
        hello("dp", dp + 4 - 8 * y)

    @pl.when(middle)
    def _():
        hello("mp", 3 - mp)
        hello("mp", 3 * (mp - 1))
        pl.semaphore_wait(barrier, 5 if with_blocks else 2)

    @pl.when(jnp.logical_not(middle))
    def _():
        hello("mp", 1 + mp // 3)
        pl.semaphore_wait(barrier, 4 if with_blocks else 1)

    return middle


def traffic_kernel(n_sums, n_lefts, n_rights, n_shards, items, *refs):
    refs = list(refs)
    take = lambda n: [refs.pop(0) for _ in range(n)]
    parts, lefts, rights = take(n_sums), take(n_lefts), take(n_rights)
    outs, shards = take(n_sums), take(n_shards)
    turned = take(n_lefts)
    line_scratch = [take(4) for _ in range(n_sums)]
    item_scratch = [take(6) for _ in items]
    middle = greet(len(items) > 0)
    sums = [LineSum(p, o, *s) for p, o, s in zip(parts, outs, line_scratch)]

    def view(shard):
        return shards[shard] if isinstance(shard, int) else shards[shard[0]].at[shard[1]]

    blocks = [
        BlockSum(turned[left], rights[right], view(shard), *scratch, by_rows, start, size)
        for (left, right, shard, by_rows, start, size), scratch in zip(items, item_scratch)
    ]

    @pl.when(jnp.logical_not(middle))
    def _():
        for one in sums:
            one.end_start()

    ready = set()

    def opening(t):
        left = items[t][0]
        if left not in ready:
            ready.add(left)
            turned[left][...] = lefts[left][...].T
        blocks[t].stage0()

    steps = [(one, k) for one in sums for k in range(one.chunks)]
    actions = []
    for t in range(len(steps) + 2):
        actions.append((steps[t] if t < len(steps) else None, steps[t - 2] if t >= 2 else None))

    def run(batch):
        @pl.when(middle)
        def _():
            for first, last in batch:
                if first is not None:
                    first[0].middle_step(first[1])
                if last is not None:
                    last[0].middle_close(last[1])

    slots = []
    count = len(blocks)
    for t in range(count + 7):
        if t < count:
            slots.append((functools.partial(opening, t), 1 if t else 0))
        if 0 <= t - 1 < count:
            slots.append((blocks[t - 1].stage1, 2 if t > 1 else 1))
        if 0 <= t - 4 < count:
            slots.append((blocks[t - 4].stage2, 2))
        if 0 <= t - 6 < count:
            slots.append((blocks[t - 6].finish, 2))
    done = 0
    for slot, weight in slots:
        slot()
        batch = actions[done : done + weight]
        done += weight
        if batch:
            run(batch)
    if actions[done:]:
        run(actions[done:])

    @pl.when(middle)
    def _():
        for one in sums:
            one.middle_finish()

    @pl.when(jnp.logical_not(middle))
    def _():
        for one in sums:
            one.end_finish()

    for block in blocks:
        block.drain()


def traffic(partials, lefts, rights, shards, items, collective_id):
    f32 = jnp.float32
    scratch = [pltpu.VMEM(left.shape[::-1], left.dtype) for left in lefts]
    for p in partials:
        scratch += [pltpu.VMEM(p.shape, f32)] * 3 + [pltpu.SemaphoreType.DMA((6, p.shape[0] // CHUNK_ROWS))]
    for left, right, _, by_rows, _, size in items:
        r, c = (lefts[left].shape[1] // 8, size) if by_rows else (size, rights[right].shape[1] // 8)
        scratch += [
            pltpu.VMEM((4, r, c), f32),
            pltpu.VMEM((4, r, c), f32),
            pltpu.VMEM((4, r // 2, c), f32),
            pltpu.VMEM((2, r // 2, c), f32),
            pltpu.SemaphoreType.DMA((10,)),
            pltpu.SemaphoreType.DMA((10,)),
        ]
    vmem = pl.BlockSpec(memory_space=pltpu.VMEM)
    return pl.pallas_call(
        functools.partial(traffic_kernel, len(partials), len(lefts), len(rights), len(shards), items),
        out_shape=[jax.ShapeDtypeStruct(p.shape, f32) for p in partials]
        + [jax.ShapeDtypeStruct(shape, f32) for shape in shards],
        in_specs=[vmem] * (len(partials) + len(lefts) + len(rights)),
        out_specs=[vmem] * (len(partials) + len(shards)),
        scratch_shapes=scratch,
        compiler_params=pltpu.CompilerParams(
            collective_id=collective_id, has_side_effects=True, vmem_limit_bytes=48 * 1024 * 1024
        ),
        name=f"traffic_{collective_id}",
    )(*partials, *lefts, *rights)


def small_kernel(n, x_ref, o_ref, held, sends, recvs):
    me = lax.axis_index("dp")
    barrier = pltpu.get_barrier_semaphore()
    for s in range(1, n):
        pl.semaphore_signal(barrier, inc=1, device_id={"dp": lax.rem(me + s, n)}, device_id_type=MESH)
    pl.semaphore_wait(barrier, n - 1)

    def copy(s):
        return remote(x_ref, held.at[me], sends.at[s], recvs.at[s], "dp", lax.rem(me + s, n))

    for s in range(1, n):
        copy(s).start()
    held[me] = x_ref[...]
    for s in range(1, n):
        copy(s).wait_recv()
    total = held[0]
    for i in range(1, n):
        total = total + held[i]
    o_ref[...] = total
    for s in range(1, n):
        copy(s).wait_send()


def small_sum(n, x, collective_id):
    vmem = pl.BlockSpec(memory_space=pltpu.VMEM)
    return pl.pallas_call(
        functools.partial(small_kernel, n),
        out_shape=jax.ShapeDtypeStruct(x.shape, x.dtype),
        in_specs=[vmem],
        out_specs=vmem,
        scratch_shapes=[
            pltpu.VMEM((n, *x.shape), x.dtype),
            pltpu.SemaphoreType.DMA((n,)),
            pltpu.SemaphoreType.DMA((n,)),
        ],
        compiler_params=pltpu.CompilerParams(collective_id=collective_id, has_side_effects=True),
        name="small_sum",
    )(x)


def split_rows(left, right, shard, size, pieces):
    step = size // pieces
    return [(left, right, shard, False, i * step, step) for i in range(pieces)]


def split_columns(left, right, shard, size, pieces):
    lanes = size // 128
    edges = [i * lanes // pieces * 128 for i in range(pieces)] + [size]
    return [(left, right, shard, True, a, b - a) for a, b in zip(edges, edges[1:])]


def rms_forward(values, norm_gain):
    inverse = lax.rsqrt(jnp.mean(values * values, axis=-1, keepdims=True) + epsilon)
    unit = values * inverse
    return (unit, inverse, (unit * norm_gain).astype(jnp.bfloat16))


def rms_backward(grad_normed, unit, inverse, norm_gain):
    grad_gain = jnp.sum(grad_normed * unit, axis=0)
    scaled = grad_normed * norm_gain
    grad_values = inverse * (scaled - unit * jnp.mean(scaled * unit, axis=-1, keepdims=True))
    return (grad_values, grad_gain)


def lagged(values, offset):
    return jnp.pad(values, ((offset, 0), (0, 0)))[: values.shape[0]]


def leading(values, offset):
    return jnp.pad(values, ((0, offset), (0, 0)))[offset:]


def conv_forward(mixed, conv_taps):
    total = jnp.zeros(mixed.shape, jnp.float32)
    for offset in range(conv_taps.shape[0]):
        total = total + conv_taps[offset] * lagged(mixed, offset)
    return total


def conv_backward(grad_conv, mixed, conv_taps):
    grad_mixed = jnp.zeros(mixed.shape, jnp.float32)
    rows_list = []
    for offset in range(conv_taps.shape[0]):
        grad_mixed = grad_mixed + conv_taps[offset] * leading(grad_conv, offset)
        rows_list.append(jnp.sum(grad_conv * lagged(mixed, offset), axis=0))
    return (grad_mixed, jnp.stack(rows_list))


def sums_over_mp(fast, partials, collective_id):
    if fast:
        return traffic(partials, [], [], [], [], collective_id)
    return [lax.psum(p, "mp") for p in partials]


def body(
    parts,
    groups,
    tokens,
    norm_gain1,
    in_weight,
    conv_taps,
    out_weight,
    norm_gain2,
    gate_weight,
    up_weight,
    down_weight,
    cotangent,
):
    length = tokens.shape[0]
    width = tokens.shape[1]
    streams = in_weight.transpose(1, 0, 2)
    inputs = tokens.astype(jnp.float32)
    unit1, inverse1, normed1 = rms_forward(inputs, norm_gain1)
    gate_b, gate_c, stream_x = [
        jnp.dot(normed1, streams[i], preferred_element_type=jnp.float32) for i in range(3)
    ]
    mixed = gate_b * stream_x
    conved = conv_forward(mixed, conv_taps)
    gated = (gate_c * conved).astype(jnp.bfloat16)
    fast = parts == 8 and groups == 4
    (branch,) = sums_over_mp(
        fast, [jnp.dot(gated, out_weight, preferred_element_type=jnp.float32)], 0
    )
    resid = inputs + branch
    unit2, inverse2, normed2 = rms_forward(resid, norm_gain2)
    gate_pre = jnp.dot(normed2, gate_weight, preferred_element_type=jnp.float32)
    up_pre = jnp.dot(normed2, up_weight, preferred_element_type=jnp.float32)
    sigmoid_gate = jax.nn.sigmoid(gate_pre)
    silu_gate = gate_pre * sigmoid_gate
    hidden = (silu_gate * up_pre).astype(jnp.bfloat16)
    partial_ffn = jnp.dot(hidden, down_weight, preferred_element_type=jnp.float32)
    grad_hidden = jnp.dot(cotangent, down_weight.T, preferred_element_type=jnp.float32)
    grad_gpre = (
        grad_hidden * up_pre * sigmoid_gate * (1.0 + gate_pre * (1.0 - sigmoid_gate))
    ).astype(jnp.bfloat16)
    grad_upre = (grad_hidden * silu_gate).astype(jnp.bfloat16)
    partial_norm2 = jnp.dot(grad_gpre, gate_weight.T, preferred_element_type=jnp.float32) + jnp.dot(
        grad_upre, up_weight.T, preferred_element_type=jnp.float32
    )
    if fast:
        rest = length // 2
        ff = hidden.shape[1]
        grad_norm2, ffn_head, summed_down, summed_gate = traffic(
            [partial_norm2, partial_ffn[:rest]],
            [hidden, normed2],
            [cotangent, grad_gpre],
            [(ff, width // parts), (width // parts, ff)],
            split_rows(0, 0, 0, ff, 2) + split_columns(1, 1, 1, ff, 2),
            1,
        )
    else:
        grad_norm2, ffn_out = lax.psum((partial_norm2, partial_ffn), "mp")
        grad_down = jnp.dot(hidden.T, cotangent, preferred_element_type=jnp.float32)
        grad_gate = jnp.dot(normed2.T, grad_gpre, preferred_element_type=jnp.float32)
        grad_up = jnp.dot(normed2.T, grad_upre, preferred_element_type=jnp.float32)
        summed_down = lax.psum_scatter(grad_down, "dp", scatter_dimension=1, tiled=True)
        summed_gate = lax.psum_scatter(grad_gate, "dp", scatter_dimension=0, tiled=True)
        summed_up = lax.psum_scatter(grad_up, "dp", scatter_dimension=0, tiled=True)
    grad_from2, grad_gain2 = rms_backward(grad_norm2, unit2, inverse2, norm_gain2)
    grad_resid = cotangent.astype(jnp.float32) + grad_from2
    resid_bf = grad_resid.astype(jnp.bfloat16)
    grad_gated = jnp.dot(resid_bf, out_weight.T, preferred_element_type=jnp.float32)
    grad_c = grad_gated * conved
    grad_conv = grad_gated * gate_c
    grad_mixed, grad_taps = conv_backward(grad_conv, mixed, conv_taps)
    grad_proj = [
        value.astype(jnp.bfloat16) for value in (grad_mixed * stream_x, grad_c, grad_mixed * gate_b)
    ]
    partial_norm1 = jnp.zeros((length, width), jnp.float32)
    for i in range(3):
        partial_norm1 += jnp.dot(grad_proj[i], streams[i].T, preferred_element_type=jnp.float32)
    if fast:
        channels = gated.shape[1]
        grad_norm1, ffn_tail, summed_up, summed_in, summed_out = traffic(
            [partial_norm1, partial_ffn[rest:]],
            [normed2, normed1, gated],
            [grad_upre, *grad_proj, resid_bf],
            [(width // parts, ff), (3, width // parts, channels), (channels, width // parts)],
            split_columns(0, 0, 0, ff, 2)
            + [(1, 1 + i, (1, i), True, 0, channels) for i in range(3)]
            + split_rows(2, 4, 2, channels, 1),
            2,
        )
        ffn_out = jnp.concatenate([ffn_head, ffn_tail])
    else:
        grad_norm1 = lax.psum(partial_norm1, "mp")
        grad_in = jnp.stack(
            [jnp.dot(normed1.T, g, preferred_element_type=jnp.float32) for g in grad_proj]
        )
        grad_out = jnp.dot(gated.T, resid_bf, preferred_element_type=jnp.float32)
        summed_in = lax.psum_scatter(grad_in, "dp", scatter_dimension=1, tiled=True)
        summed_out = lax.psum_scatter(grad_out, "dp", scatter_dimension=1, tiled=True)
    block_out = (resid + ffn_out).astype(jnp.bfloat16)
    grad_from1, grad_gain1 = rms_backward(grad_norm1, unit1, inverse1, norm_gain1)
    input_grad = (grad_resid + grad_from1).astype(jnp.bfloat16)
    if fast:
        small = jnp.concatenate(
            [grad_gain1.reshape(-1, 128), grad_gain2.reshape(-1, 128), grad_taps.reshape(-1, 128)]
        )
        count = small.shape[0]
        small = small_sum(parts, jnp.pad(small, ((0, -count % 8), (0, 0))), 3)
        rows = width // 128
        total_gain1 = small[:rows].reshape(-1)
        total_gain2 = small[rows : 2 * rows].reshape(-1)
        total_taps = small[2 * rows : count].reshape(grad_taps.shape)
    else:
        total_gain1, total_taps, total_gain2 = lax.psum((grad_gain1, grad_taps, grad_gain2), "dp")
    return (
        block_out,
        input_grad,
        total_gain1,
        summed_in.transpose(1, 0, 2),
        total_taps,
        summed_out,
        total_gain2,
        summed_gate,
        summed_up,
        summed_down,
    )


def solution(mesh):
    in_specs = (
        P("dp", None),
        P(),
        P(None, None, "mp"),
        P(None, "mp"),
        P("mp", None),
        P(),
        P(None, "mp"),
        P(None, "mp"),
        P("mp", None),
        P("dp", None),
    )
    out_specs = (
        P("dp", None),
        P("dp", None),
        P(),
        P("dp", None, "mp"),
        P(None, "mp"),
        P("mp", "dp"),
        P(),
        P("dp", "mp"),
        P("dp", "mp"),
        P("mp", "dp"),
    )
    local = functools.partial(body, mesh.shape["dp"], mesh.shape["mp"])
    return jax.shard_map(local, mesh=mesh, in_specs=in_specs, out_specs=out_specs, check_vma=False)
```

```python
import functools

import jax
import jax.numpy as jnp
from jax import lax
from jax.experimental import pallas as pl
from jax.experimental.pallas import tpu as pltpu
from jax.sharding import PartitionSpec as P

epsilon = 1e-05
MESH = pl.DeviceIdType.MESH
CHUNK_ROWS = 16


def remote(src, dst, send, recv, axis, index):
    return pltpu.make_async_remote_copy(
        src_ref=src,
        dst_ref=dst,
        send_sem=send,
        recv_sem=recv,
        device_id={axis: index},
        device_id_type=MESH,
    )


class LineSum:
    def __init__(self, part, out, near, across, total, sems):
        self.part, self.out = part, out
        self.near, self.across, self.total = near, across, total
        self.sems = sems
        self.me = lax.axis_index("mp")
        self.rows = CHUNK_ROWS
        self.chunks = part.shape[0] // CHUNK_ROWS

    def at(self, ref, k):
        return ref.at[pl.ds(k * self.rows, self.rows), :]

    def inward(self, k):
        return remote(
            self.at(self.part, k), self.at(self.near, k),
            self.sems.at[0, k], self.sems.at[1, k], "mp", 1 + self.me // 3,
        )

    def swap(self, k):
        return remote(
            self.at(self.near, k), self.at(self.across, k),
            self.sems.at[2, k], self.sems.at[3, k], "mp", 3 - self.me,
        )

    def outward(self, k):
        return remote(
            self.at(self.total, k), self.at(self.total, k),
            self.sems.at[4, k], self.sems.at[5, k], "mp", (3 * self.me + 1) % 4,
        )

    def end_start(self):
        for k in range(self.chunks):
            self.inward(k).start()

    def middle_step(self, k):
        self.inward(k).wait_recv()
        rows = pl.ds(k * self.rows, self.rows)
        self.near[rows, :] = self.near[rows, :] + self.part[rows, :]
        self.swap(k).start()

    def middle_close(self, k):
        self.swap(k).wait_recv()
        rows = pl.ds(k * self.rows, self.rows)
        self.total[rows, :] = self.near[rows, :] + self.across[rows, :]
        self.outward(k).start()
        self.out[rows, :] = self.total[rows, :]

    def end_finish(self):
        for k in range(self.chunks):
            self.outward(k).wait_recv()
            rows = pl.ds(k * self.rows, self.rows)
            self.out[rows, :] = self.total[rows, :]
        for k in range(self.chunks):
            self.inward(k).wait_send()

    def middle_finish(self):
        for k in range(self.chunks):
            self.swap(k).wait_send()
            self.outward(k).wait_send()


class BlockSum:
    def __init__(self, left, right, out, mine, first, second, third, sends, recvs, by_rows, start, size):
        self.left, self.right, self.out, self.mine = left, right, out, mine
        self.first, self.second, self.third = first, second, third
        self.sends, self.recvs = sends, recvs
        self.by_rows, self.start, self.size = by_rows, start, size
        me = lax.axis_index("dp")
        self.y, self.x, self.c = me // 4, (me // 2) % 2, me % 2
        self.to_core = me + 1 - 2 * self.c
        self.to_x = me + 2 - 4 * self.x
        self.to_y = me + 4 - 8 * self.y
        self.block = first.shape[1]
        self.half = self.block // 2

    def produce(self, j):
        if self.by_rows:
            rows = pl.ds(pl.multiple_of(j * self.block, self.block), self.block)
            columns = pl.ds(self.start, self.size)
        else:
            width = self.first.shape[2]
            rows = pl.ds(self.start, self.size)
            columns = pl.ds(pl.multiple_of(j * width, width), width)
        return jnp.dot(self.left[rows, :], self.right[:, columns], preferred_element_type=jnp.float32)

    def target(self, h):
        if self.by_rows:
            return (pl.ds(h * self.half, self.half), pl.ds(self.start, self.size))
        return (pl.ds(self.start + h * self.half, self.half), slice(None))

    def part(self, h):
        return pl.ds(h * self.half, self.half)

    def copy0(self, q):
        return remote(
            self.mine.at[q], self.first.at[q],
            self.sends.at[q], self.recvs.at[q], "dp", self.to_core,
        )

    def copy1(self, n):
        if n < 2:
            src, dst = self.first.at[2 * n + 1 - self.x, self.part(0)], self.to_x
        else:
            src, dst = self.first.at[2 * (1 - self.y) + n - 2, self.part(1)], self.to_y
        return remote(src, self.second.at[n], self.sends.at[4 + n], self.recvs.at[4 + n], "dp", dst)

    def copy2(self, h):
        if h == 0:
            src, dst = self.second.at[1 - self.y], self.to_y
        else:
            src, dst = self.second.at[3 - self.x], self.to_x
        return remote(src, self.third.at[h], self.sends.at[8 + h], self.recvs.at[8 + h], "dp", dst)

    def stage0(self):
        for q in range(4):
            self.mine[q] = self.produce(2 * q + 1 - self.c)
            self.copy0(q).start()

    def stage1(self):
        for q in range(4):
            self.copy0(q).wait_recv()
            self.first[q] = self.first[q] + self.produce(2 * q + self.c)
        for n in (0, 2, 1, 3):
            self.copy1(n).start()

    def stage2(self):
        for n in range(4):
            self.copy1(n).wait_recv()
            if n < 2:
                mine = self.first[2 * n + self.x, self.part(0)]
            else:
                mine = self.first[2 * self.y + n - 2, self.part(1)]
            self.second[n] = self.second[n] + mine
        for h in range(2):
            self.copy2(h).start()

    def finish(self):
        for h in range(2):
            self.copy2(h).wait_recv()
            mine = self.second[self.y] if h == 0 else self.second[2 + self.x]
            self.out[self.target(h)] = mine + self.third[h]

    def drain(self):
        for q in range(4):
            self.copy0(q).wait_send()
            self.copy1(q).wait_send()
        for h in range(2):
            self.copy2(h).wait_send()


def greet(peers):
    barrier = pltpu.get_barrier_semaphore()
    mp, dp = lax.axis_index("mp"), lax.axis_index("dp")
    middle = (mp == 1) | (mp == 2)

    def hello(axis, index):
        pl.semaphore_signal(barrier, inc=1, device_id={axis: index}, device_id_type=MESH)

    if peers == 7:
        for s in range(1, 8):
            hello("dp", lax.rem(dp + s, 8))
    elif peers == 3:
        y, x, c = dp // 4, (dp // 2) % 2, dp % 2
        hello("dp", dp + 1 - 2 * c)
        hello("dp", dp + 2 - 4 * x)
        hello("dp", dp + 4 - 8 * y)

    @pl.when(middle)
    def _():
        hello("mp", 3 - mp)
        hello("mp", 3 * (mp - 1))
        pl.semaphore_wait(barrier, 2 + peers)

    @pl.when(jnp.logical_not(middle))
    def _():
        hello("mp", 1 + mp // 3)
        pl.semaphore_wait(barrier, 1 + peers)

    return middle


class SmallSum:
    def __init__(self, unit, given, out, own, held, sends, recvs):
        self.unit, self.given, self.out = unit, given, out
        self.own, self.held, self.sends, self.recvs = own, held, sends, recvs
        self.me = lax.axis_index("dp")

    def copy(self, s):
        return remote(
            self.own, self.held.at[self.me], self.sends.at[s], self.recvs.at[s],
            "dp", lax.rem(self.me + s, 8),
        )

    def begin(self, grad):
        gain = jnp.sum(grad[...] * self.unit[...], axis=0, keepdims=True)
        self.own[...] = self.given[...]
        for i in range(gain.shape[1] // 128):
            self.own[i : i + 1, :] = gain[:, i * 128 : (i + 1) * 128]
        for s in range(1, 8):
            self.copy(s).start()
        self.held[self.me] = self.own[...]

    def end(self):
        for s in range(1, 8):
            self.copy(s).wait_recv()
        total = self.held[0]
        for i in range(1, 8):
            total = total + self.held[i]
        self.out[...] = total
        for s in range(1, 8):
            self.copy(s).wait_send()


def traffic_kernel(n_sums, n_lefts, n_rights, n_shards, items, tail, *refs):
    refs = list(refs)
    take = lambda n: [refs.pop(0) for _ in range(n)]
    parts, lefts, rights = take(n_sums), take(n_lefts), take(n_rights)
    extra = take(2) if tail else []
    outs, shards = take(n_sums), take(n_shards)
    extra += take(1) if tail else []
    turned = take(n_lefts)
    line_scratch = [take(4) for _ in range(n_sums)]
    item_scratch = [take(6) for _ in items]
    small = SmallSum(*extra, *take(4)) if tail else None
    middle = greet(7 if tail else 3 if items else 0)
    sums = [LineSum(p, o, *s) for p, o, s in zip(parts, outs, line_scratch)]

    def view(shard):
        return shards[shard] if isinstance(shard, int) else shards[shard[0]].at[shard[1]]

    blocks = [
        BlockSum(turned[left], rights[right], view(shard), *scratch, by_rows, start, size)
        for (left, right, shard, by_rows, start, size), scratch in zip(items, item_scratch)
    ]

    @pl.when(jnp.logical_not(middle))
    def _():
        for one in sums:
            one.end_start()

    ready = set()

    def opening(t):
        left = items[t][0]
        if left not in ready:
            ready.add(left)
            turned[left][...] = lefts[left][...].T
        blocks[t].stage0()

    steps = [(one, k) for one in sums for k in range(one.chunks)]
    actions = []
    for t in range(len(steps) + 2):
        actions.append((steps[t] if t < len(steps) else None, steps[t - 2] if t >= 2 else None))

    def run(batch):
        @pl.when(middle)
        def _():
            for first, last in batch:
                if first is not None:
                    first[0].middle_step(first[1])
                if last is not None:
                    last[0].middle_close(last[1])

    slots = []
    count = len(blocks)
    for t in range(count + 4):
        if t < count:
            slots.append((functools.partial(opening, t), 1 if t else 0))
        if 0 <= t - 1 < count:
            slots.append((blocks[t - 1].stage1, 1))
        if 0 <= t - 4 < count:
            slots.append((blocks[t - 4].stage2, 2))
        if 0 <= t - 6 < count:
            slots.append((blocks[t - 6].finish, 1))
    done = 0
    for slot, weight in slots:
        slot()
        batch = actions[done : done + weight]
        done += weight
        if batch:
            run(batch)
    if actions[done:]:
        run(actions[done:])

    @pl.when(middle)
    def _():
        for one in sums:
            one.middle_finish()

    @pl.when(jnp.logical_not(middle))
    def _():
        for one in sums:
            one.end_finish()

    if small is not None:
        small.begin(outs[0])
    for block in blocks[max(count - 2, 0) :]:
        block.finish()
    if small is not None:
        small.end()
    for block in blocks:
        block.drain()


def traffic(partials, lefts, rights, shards, items, collective_id, tail=()):
    f32 = jnp.float32
    scratch = [pltpu.VMEM(left.shape[::-1], left.dtype) for left in lefts]
    for p in partials:
        scratch += [pltpu.VMEM(p.shape, f32)] * 3 + [pltpu.SemaphoreType.DMA((6, p.shape[0] // CHUNK_ROWS))]
    for left, right, _, by_rows, _, size in items:
        r, c = (lefts[left].shape[1] // 8, size) if by_rows else (size, rights[right].shape[1] // 8)
        scratch += [
            pltpu.VMEM((4, r, c), f32),
            pltpu.VMEM((4, r, c), f32),
            pltpu.VMEM((4, r // 2, c), f32),
            pltpu.VMEM((2, r // 2, c), f32),
            pltpu.SemaphoreType.DMA((10,)),
            pltpu.SemaphoreType.DMA((10,)),
        ]
    for _, given in zip(tail[:1], tail[1:]):
        scratch += [
            pltpu.VMEM(given.shape, f32),
            pltpu.VMEM((8, *given.shape), f32),
            pltpu.SemaphoreType.DMA((8,)),
            pltpu.SemaphoreType.DMA((8,)),
        ]
    vmem = pl.BlockSpec(memory_space=pltpu.VMEM)
    return pl.pallas_call(
        functools.partial(
            traffic_kernel, len(partials), len(lefts), len(rights), len(shards), items, len(tail) > 0
        ),
        out_shape=[jax.ShapeDtypeStruct(p.shape, f32) for p in partials]
        + [jax.ShapeDtypeStruct(shape, f32) for shape in shards]
        + [jax.ShapeDtypeStruct(given.shape, f32) for given in tail[1:]],
        in_specs=[vmem] * (len(partials) + len(lefts) + len(rights) + len(tail)),
        out_specs=[vmem] * (len(partials) + len(shards) + len(tail[1:])),
        scratch_shapes=scratch,
        compiler_params=pltpu.CompilerParams(
            collective_id=collective_id, has_side_effects=True, vmem_limit_bytes=48 * 1024 * 1024
        ),
        name=f"traffic_{collective_id}",
    )(*partials, *lefts, *rights, *tail)


def hand_over_kernel(n, *refs):
    small, gain1, gain2, taps = refs[n], refs[-3], refs[-2], refs[-1]
    for i in range(n):
        refs[n + 1 + i][...] = refs[i][...]
    rows = gain1.shape[1] // 128
    for i in range(rows):
        gain1[:, i * 128 : (i + 1) * 128] = small[i : i + 1, :]
        gain2[:, i * 128 : (i + 1) * 128] = small[rows + i : rows + i + 1, :]
    per = taps.shape[1] // 128
    for k in range(taps.shape[0]):
        for i in range(per):
            at = 2 * rows + k * per + i
            taps[k : k + 1, i * 128 : (i + 1) * 128] = small[at : at + 1, :]


def hand_over(shards, small, width, taps_shape):
    vmem = pl.BlockSpec(memory_space=pltpu.VMEM)
    shapes = [x.shape for x in shards] + [(1, width), (1, width), taps_shape]
    return pl.pallas_call(
        functools.partial(hand_over_kernel, len(shards)),
        out_shape=[jax.ShapeDtypeStruct(shape, jnp.float32) for shape in shapes],
        in_specs=[vmem] * (len(shards) + 1),
        out_specs=[vmem] * len(shapes),
        name="hand_over",
    )(*shards, small)


def split_rows(left, right, shard, size, pieces):
    step = size // pieces
    return [(left, right, shard, False, i * step, step) for i in range(pieces)]


def split_columns(left, right, shard, size, pieces):
    lanes = size // 128
    edges = [i * lanes // pieces * 128 for i in range(pieces)] + [size]
    return [(left, right, shard, True, a, b - a) for a, b in zip(edges, edges[1:])]


def rms_forward(values, norm_gain):
    inverse = lax.rsqrt(jnp.mean(values * values, axis=-1, keepdims=True) + epsilon)
    unit = values * inverse
    return (unit, inverse, (unit * norm_gain).astype(jnp.bfloat16))


def rms_backward(grad_normed, unit, inverse, norm_gain):
    grad_gain = jnp.sum(grad_normed * unit, axis=0)
    scaled = grad_normed * norm_gain
    grad_values = inverse * (scaled - unit * jnp.mean(scaled * unit, axis=-1, keepdims=True))
    return (grad_values, grad_gain)


def lagged(values, offset):
    return jnp.pad(values, ((offset, 0), (0, 0)))[: values.shape[0]]


def leading(values, offset):
    return jnp.pad(values, ((0, offset), (0, 0)))[offset:]


def conv_forward(mixed, conv_taps):
    total = jnp.zeros(mixed.shape, jnp.float32)
    for offset in range(conv_taps.shape[0]):
        total = total + conv_taps[offset] * lagged(mixed, offset)
    return total


def conv_backward(grad_conv, mixed, conv_taps):
    grad_mixed = jnp.zeros(mixed.shape, jnp.float32)
    rows_list = []
    for offset in range(conv_taps.shape[0]):
        grad_mixed = grad_mixed + conv_taps[offset] * leading(grad_conv, offset)
        rows_list.append(jnp.sum(grad_conv * lagged(mixed, offset), axis=0))
    return (grad_mixed, jnp.stack(rows_list))


def sums_over_mp(fast, partials, collective_id):
    if fast:
        return traffic(partials, [], [], [], [], collective_id)
    return [lax.psum(p, "mp") for p in partials]


def body(
    parts,
    groups,
    tokens,
    norm_gain1,
    in_weight,
    conv_taps,
    out_weight,
    norm_gain2,
    gate_weight,
    up_weight,
    down_weight,
    cotangent,
):
    length = tokens.shape[0]
    width = tokens.shape[1]
    streams = in_weight.transpose(1, 0, 2)
    inputs = tokens.astype(jnp.float32)
    unit1, inverse1, normed1 = rms_forward(inputs, norm_gain1)
    gate_b, gate_c, stream_x = [
        jnp.dot(normed1, streams[i], preferred_element_type=jnp.float32) for i in range(3)
    ]
    mixed = gate_b * stream_x
    conved = conv_forward(mixed, conv_taps)
    gated = (gate_c * conved).astype(jnp.bfloat16)
    fast = parts == 8 and groups == 4
    (branch,) = sums_over_mp(
        fast, [jnp.dot(gated, out_weight, preferred_element_type=jnp.float32)], 0
    )
    resid = inputs + branch
    unit2, inverse2, normed2 = rms_forward(resid, norm_gain2)
    gate_pre = jnp.dot(normed2, gate_weight, preferred_element_type=jnp.float32)
    up_pre = jnp.dot(normed2, up_weight, preferred_element_type=jnp.float32)
    sigmoid_gate = jax.nn.sigmoid(gate_pre)
    silu_gate = gate_pre * sigmoid_gate
    hidden = (silu_gate * up_pre).astype(jnp.bfloat16)
    partial_ffn = jnp.dot(hidden, down_weight, preferred_element_type=jnp.float32)
    grad_hidden = jnp.dot(cotangent, down_weight.T, preferred_element_type=jnp.float32)
    grad_gpre = (
        grad_hidden * up_pre * sigmoid_gate * (1.0 + gate_pre * (1.0 - sigmoid_gate))
    ).astype(jnp.bfloat16)
    grad_upre = (grad_hidden * silu_gate).astype(jnp.bfloat16)
    partial_norm2 = jnp.dot(grad_gpre, gate_weight.T, preferred_element_type=jnp.float32) + jnp.dot(
        grad_upre, up_weight.T, preferred_element_type=jnp.float32
    )
    if fast:
        rest = length // 2
        ff = hidden.shape[1]
        grad_norm2, ffn_head, summed_down, summed_gate = traffic(
            [partial_norm2, partial_ffn[:rest]],
            [hidden, normed2],
            [cotangent, grad_gpre],
            [(ff, width // parts), (width // parts, ff)],
            split_rows(0, 0, 0, ff, 4) + split_columns(1, 1, 1, ff, 4),
            1,
        )
    else:
        grad_norm2, ffn_out = lax.psum((partial_norm2, partial_ffn), "mp")
        grad_down = jnp.dot(hidden.T, cotangent, preferred_element_type=jnp.float32)
        grad_gate = jnp.dot(normed2.T, grad_gpre, preferred_element_type=jnp.float32)
        grad_up = jnp.dot(normed2.T, grad_upre, preferred_element_type=jnp.float32)
        summed_down = lax.psum_scatter(grad_down, "dp", scatter_dimension=1, tiled=True)
        summed_gate = lax.psum_scatter(grad_gate, "dp", scatter_dimension=0, tiled=True)
        summed_up = lax.psum_scatter(grad_up, "dp", scatter_dimension=0, tiled=True)
    grad_from2, grad_gain2 = rms_backward(grad_norm2, unit2, inverse2, norm_gain2)
    grad_resid = cotangent.astype(jnp.float32) + grad_from2
    resid_bf = grad_resid.astype(jnp.bfloat16)
    grad_gated = jnp.dot(resid_bf, out_weight.T, preferred_element_type=jnp.float32)
    grad_c = grad_gated * conved
    grad_conv = grad_gated * gate_c
    grad_mixed, grad_taps = conv_backward(grad_conv, mixed, conv_taps)
    grad_proj = [
        value.astype(jnp.bfloat16) for value in (grad_mixed * stream_x, grad_c, grad_mixed * gate_b)
    ]
    partial_norm1 = jnp.zeros((length, width), jnp.float32)
    for i in range(3):
        partial_norm1 += jnp.dot(grad_proj[i], streams[i].T, preferred_element_type=jnp.float32)
    if fast:
        channels = gated.shape[1]
        small = jnp.concatenate(
            [
                jnp.zeros((width // 128, 128), jnp.float32),
                grad_gain2.reshape(-1, 128),
                grad_taps.reshape(-1, 128),
            ]
        )
        small = jnp.pad(small, ((0, -small.shape[0] % 8), (0, 0)))
        grad_norm1, ffn_tail, summed_up, summed_in, summed_out, small = traffic(
            [partial_norm1, partial_ffn[rest:]],
            [normed2, normed1, gated],
            [grad_upre, *grad_proj, resid_bf],
            [(width // parts, ff), (3, width // parts, channels), (channels, width // parts)],
            split_columns(0, 0, 0, ff, 4)
            + [(1, 1 + i, (1, i), True, 0, channels) for i in range(3)]
            + split_rows(2, 4, 2, channels, 1),
            2,
            (unit1, small),
        )
        ffn_out = jnp.concatenate([ffn_head, ffn_tail])
    else:
        grad_norm1 = lax.psum(partial_norm1, "mp")
        grad_in = jnp.stack(
            [jnp.dot(normed1.T, g, preferred_element_type=jnp.float32) for g in grad_proj]
        )
        grad_out = jnp.dot(gated.T, resid_bf, preferred_element_type=jnp.float32)
        summed_in = lax.psum_scatter(grad_in, "dp", scatter_dimension=1, tiled=True)
        summed_out = lax.psum_scatter(grad_out, "dp", scatter_dimension=1, tiled=True)
    block_out = (resid + ffn_out).astype(jnp.bfloat16)
    grad_from1, grad_gain1 = rms_backward(grad_norm1, unit1, inverse1, norm_gain1)
    input_grad = (grad_resid + grad_from1).astype(jnp.bfloat16)
    if fast:
        shards = [summed_in, summed_out, summed_gate, summed_up, summed_down]
        *shards, total_gain1, total_gain2, total_taps = hand_over(shards, small, width, grad_taps.shape)
        summed_in, summed_out, summed_gate, summed_up, summed_down = shards
        total_gain1, total_gain2 = total_gain1.reshape(-1), total_gain2.reshape(-1)
    else:
        total_gain1, total_taps, total_gain2 = lax.psum((grad_gain1, grad_taps, grad_gain2), "dp")
    return (
        block_out,
        input_grad,
        total_gain1,
        summed_in.transpose(1, 0, 2),
        total_taps,
        summed_out,
        total_gain2,
        summed_gate,
        summed_up,
        summed_down,
    )


def solution(mesh):
    in_specs = (
        P("dp", None),
        P(),
        P(None, None, "mp"),
        P(None, "mp"),
        P("mp", None),
        P(),
        P(None, "mp"),
        P(None, "mp"),
        P("mp", None),
        P("dp", None),
    )
    out_specs = (
        P("dp", None),
        P("dp", None),
        P(),
        P("dp", None, "mp"),
        P(None, "mp"),
        P("mp", "dp"),
        P(),
        P("dp", "mp"),
        P("dp", "mp"),
        P("mp", "dp"),
    )
    local = functools.partial(body, mesh.shape["dp"], mesh.shape["mp"])
    return jax.shard_map(local, mesh=mesh, in_specs=in_specs, out_specs=out_specs, check_vma=False)
```
